32 devices in a mesh: dp: 2 (over y), seq: 16 (over z, x, core).
Axes of the slice: x: 2, y: 2, z: 4, core: 2. Of those that a mesh axis runs over, the one named last changes fastest.
Arguments:
- inputs: bfloat16 [2, 2176, 6144], P('dp', 'seq'), may hold values from -6 to 6
- w_project: bfloat16 [6144, 3, 128], P(('dp', 'seq')), may hold values from -0.078125 to 0.078125
- w_output: bfloat16 [6144, 128], P(('dp', 'seq')), may hold values from -0.078125 to 0.078125
- norm_gain: float32 [128], replicated, may hold values from 0.1 to 1.9
- out_grad: bfloat16 [2, 2176, 6144], P('dp', 'seq'), may hold values from -6 to 6
Outputs:
- input_grad: bfloat16 [2, 2176, 6144], P('dp', 'seq')
The draws below stay inside these ranges and needn't reach their ends.
All inputs are finite; a program needn't handle non-finite values.
Results may differ from the reference program's by a relative error of at most 0.025.
Values may be sent and summed in bfloat16 or wider, within the bound.
A program may use at most 64 MiB of HBM per device.

```python
import jax
import jax.numpy as jnp
from jax import lax

D = 6144
HEAD = 128
TOK_DEV = 136
LENGTH = 2176
BATCH = 2


def block_scale(own_key, extent, cuts, least, largest):
    factor_of, own = 1.0, jax.random.fold_in(own_key, 6)
    for dim, blocks in cuts:
        steps = jnp.exp(jax.random.uniform(jax.random.fold_in(own, dim), (blocks,), jnp.float32, least / len(cuts), largest / len(cuts)))
        factor_of = factor_of * jnp.repeat(steps, extent[dim] // blocks).reshape([-1 if axis == dim else 1 for axis in range(len(extent))])
    return factor_of


def centred(own_key, dims, scale, most, split=(), dtype=jnp.bfloat16):
    entries = jax.random.normal(own_key, dims, jnp.float32) * scale
    if len(split) > 0:
        entries = block_scale(own_key, dims, split, -0.22, 0.18) * entries
    return jnp.clip(entries, min=-most, max=most).astype(dtype)


def setup_inputs(seed: int = 0) -> dict:
    keys = jax.random.split(jax.random.key(seed), 6)
    return {
        "inputs": centred(keys[0], (BATCH, LENGTH, D), 1.0, 6.0, ((0, 2), (1, 16))),
        "w_project": centred(keys[1], (D, 3, HEAD), D ** -0.5, 0.078125, ((0, 32),)),
        "w_output": centred(keys[2], (D, HEAD), D ** -0.5, 0.078125, ((0, 32),)),
        "norm_gain": jnp.clip(1.0 + 0.18 * jax.random.normal(keys[3], (HEAD,), jnp.float32), 0.1, 1.9),
        "out_grad": centred(keys[4], (BATCH, LENGTH, D), 1.0, 6.0, ((0, 2), (1, 16))),
    }


def block_pass(tokens, grads_in, flat_proj, w_output, norm_gain):
    projected = jnp.dot(tokens, flat_proj, preferred_element_type=jnp.float32).astype(jnp.bfloat16)
    blocks = tokens.shape[0] // TOK_DEV
    queries = projected[:, :HEAD].reshape(blocks, TOK_DEV, HEAD).astype(jnp.float32)
    key_rows = projected[:, HEAD:2 * HEAD].reshape(blocks, TOK_DEV, HEAD).astype(jnp.float32)
    value_rows = projected[:, 2 * HEAD:].reshape(blocks, TOK_DEV, HEAD).astype(jnp.float32)
    causal = jnp.tril(jnp.ones((TOK_DEV, TOK_DEV), jnp.float32))
    scores = (jnp.einsum('btd,bsd->bts', queries, key_rows) * causal).astype(jnp.bfloat16).astype(jnp.float32)
    intra_part = jnp.einsum('bts,bsd->btd', scores, value_rows)
    local_state = jnp.einsum('bsk,bsv->bkv', key_rows, value_rows)
    prior_state = (jnp.cumsum(local_state, axis=0) - local_state).astype(jnp.bfloat16).astype(jnp.float32)
    attended = intra_part + jnp.einsum('btk,bkv->btv', queries, prior_state)
    inv_rms = lax.rsqrt(lax.optimization_barrier(jnp.mean(attended * attended, axis=-1, keepdims=True)) + 1e-06)
    head_grad = jnp.dot(grads_in, w_output, preferred_element_type=jnp.float32).reshape(blocks, TOK_DEV, HEAD)
    scaled = norm_gain * head_grad
    attn_grad = inv_rms * scaled - attended * inv_rms ** 3 * lax.optimization_barrier(jnp.mean(attended * scaled, axis=-1, keepdims=True))
    attn_grad = attn_grad.astype(jnp.bfloat16).astype(jnp.float32)
    prob_grad = (jnp.einsum('btv,bsv->bts', attn_grad, value_rows) * causal).astype(jnp.bfloat16).astype(jnp.float32)
    local_grad = jnp.einsum('btk,btv->bkv', queries, attn_grad)
    later_state = (jnp.flip(jnp.cumsum(jnp.flip(local_grad, 0), axis=0), 0) - local_grad).astype(jnp.bfloat16).astype(jnp.float32)
    query_grad = jnp.einsum('bts,bsk->btk', prob_grad, key_rows) + jnp.einsum('btv,bkv->btk', attn_grad, prior_state)
    key_grad = jnp.einsum('bts,btk->bsk', prob_grad, queries) + jnp.einsum('bsv,bkv->bsk', value_rows, later_state)
    value_grad = jnp.einsum('bts,btv->bsv', scores, attn_grad) + jnp.einsum('bsk,bkv->bsv', key_rows, later_state)
    joined = jnp.concatenate([query_grad, key_grad, value_grad], axis=-1).astype(jnp.bfloat16)
    joined = joined.reshape(tokens.shape[0], 3 * HEAD)
    result = lax.dot_general(joined, flat_proj, (((1,), (1,)), ((), ())), preferred_element_type=jnp.float32)
    return result.astype(jnp.bfloat16)

def reference(inputs, w_project, w_output, norm_gain, out_grad):
    flat_proj = w_project.reshape(D, 3 * HEAD)

    def one_sequence(pair):
        return block_pass(pair[0], pair[1], flat_proj, w_output, norm_gain)
    return lax.map(one_sequence, (inputs, out_grad))
```

```python
import functools

import jax
import jax.numpy as jnp
from jax import lax
from jax.experimental import pallas as pl
from jax.experimental.pallas import tpu as pltpu
from jax.sharding import PartitionSpec as P


def contract(left, right, left_dim, right_dim):
    return lax.dot_general(
        left, right, (((left_dim,), (right_dim,)), ((), ())), preferred_element_type=jnp.float32
    )


def other_blocks(local, reverse):
    every = lax.all_gather(local[None].astype(jnp.bfloat16), "seq", axis=0, tiled=True).astype(
        jnp.float32
    )
    own_index = lax.axis_index("seq")
    rank_list = jnp.arange(every.shape[0], dtype=jnp.int32)
    if reverse:
        selected = rank_list > own_index
    else:
        selected = rank_list < own_index
    return jnp.sum(jnp.where(selected[:, None, None], every, 0.0), axis=0)


def per_device_plain(inputs, w_project, w_output, norm_gain, out_grad):
    proj_full, out_full = (
        lax.all_gather(w_project, ("dp", "seq"), axis=0, tiled=True),
        lax.all_gather(w_output, ("dp", "seq"), axis=0, tiled=True),
    )
    width = proj_full.shape[0]
    head = proj_full.shape[2]
    flat_proj = proj_full.reshape(width, 3 * head)
    tokens = inputs[0]
    grads_in = out_grad[0]
    count = tokens.shape[0]
    projected = jnp.dot(tokens, flat_proj, preferred_element_type=jnp.float32).astype(jnp.bfloat16)
    queries = projected[:, :head]
    key_rows = projected[:, head : 2 * head]
    value_rows = projected[:, 2 * head :]
    row_ids = lax.broadcasted_iota(jnp.int32, (count, count), 0)
    col_ids = lax.broadcasted_iota(jnp.int32, (count, count), 1)
    causal = row_ids >= col_ids
    scores = jnp.where(causal, contract(queries, key_rows, 1, 1), 0.0).astype(jnp.bfloat16)
    intra_part = jnp.dot(scores, value_rows, preferred_element_type=jnp.float32)
    local_state = contract(key_rows, value_rows, 0, 0)
    prior_state = other_blocks(local_state, False).astype(jnp.bfloat16)
    attended = intra_part + jnp.dot(queries, prior_state, preferred_element_type=jnp.float32)
    inv_rms = lax.rsqrt(jnp.mean(attended * attended, axis=-1, keepdims=True) + 1e-06)
    head_grad = jnp.dot(grads_in, out_full, preferred_element_type=jnp.float32)
    scaled = norm_gain * head_grad
    attn_grad = inv_rms * scaled - attended * inv_rms**3 * jnp.mean(
        attended * scaled, axis=-1, keepdims=True
    )
    attn_grad = attn_grad.astype(jnp.bfloat16)
    prob_grad = jnp.where(causal, contract(attn_grad, value_rows, 1, 1), 0.0).astype(jnp.bfloat16)
    local_grad = contract(queries, attn_grad, 0, 0)
    later_state = other_blocks(local_grad, True).astype(jnp.bfloat16)
    query_grad = jnp.dot(prob_grad, key_rows, preferred_element_type=jnp.float32) + contract(
        attn_grad, prior_state, 1, 1
    )
    key_grad = contract(prob_grad, queries, 0, 0) + contract(value_rows, later_state, 1, 1)
    value_grad = contract(scores, attn_grad, 0, 0) + jnp.dot(
        key_rows, later_state, preferred_element_type=jnp.float32
    )
    joined = jnp.concatenate([query_grad, key_grad, value_grad], axis=-1).astype(jnp.bfloat16)
    result = contract(joined, flat_proj, 1, 1).astype(jnp.bfloat16)
    return result[None]


CORES = 2
WIDE = 2
PIECES = 2
MESH = pl.DeviceIdType.MESH


def fused_kernel(
    planes, x_hbm, g_hbm, w_hbm, gain_ref, out_hbm,
    xv, gv, wbuf, ob, st_send, st_in, sum_send, sum_in, acc,
    load_sem, own_sem, out_sem, recv_sem, send_sem, st_rs, st_ss, sum_rs, sum_ss,
):
    y = lax.axis_index("dp")
    seq = lax.axis_index("seq")
    core = seq % CORES
    x = (seq // CORES) % WIDE
    z = seq // (CORES * WIDE)
    head = st_send.shape[-1]
    count, width = xv.shape
    devices = wbuf.shape[1]
    rows = wbuf.shape[2]
    ya, xa = (y + core) % 2, (x + 1 - core) % 2
    yb, xb = (y + 1 - core) % 2, (x + core) % 2

    def dev(yy, zz, xx, cc):
        return (yy, (zz * WIDE + xx) * CORES + cc)

    def chip(yy, zz, xx):
        return (yy * planes + zz) * WIDE + xx

    x_load = pltpu.make_async_copy(x_hbm, xv, load_sem.at[0])
    g_load = pltpu.make_async_copy(g_hbm, gv, load_sem.at[1])
    me = chip(y, z, x) * CORES + core
    own = [
        pltpu.make_async_copy(w_hbm.at[p], wbuf.at[p, me], own_sem.at[p]) for p in range(PIECES)
    ]
    for copy in own:
        copy.start()
    x_load.start()
    g_load.start()

    barrier = pltpu.get_barrier_semaphore()
    near = [
        dev(y, z, x, 1 - core),
        dev(y, z, 1 - x, core),
        dev(y, z, 1 - x, 1 - core),
        dev(1 - y, z, x, core),
    ] + [dev(y, (z + dz) % planes, x, core) for dz in range(1, planes)]
    for other in near:
        pl.semaphore_signal(barrier, inc=1, device_id=other, device_id_type=MESH)
    pl.semaphore_wait(barrier, len(near))

    def shard_copy(way, p, origin, target):
        slot = wbuf.at[p, origin * CORES + core]
        kind = 1 if way == 4 else 0
        return pltpu.make_async_remote_copy(
            src_ref=slot,
            dst_ref=slot,
            send_sem=send_sem.at[way, p, origin],
            recv_sem=recv_sem.at[kind, p, origin],
            device_id=target,
            device_id_type=MESH,
        )

    targets = [
        dev(ya, z, xa, core),
        dev(y, lax.rem(z + 1, planes), x, core),
        dev(y, lax.rem(z + planes - 1, planes), x, core),
        dev(yb, z, xb, core),
        dev(y, z, x, 1 - core),
    ]
    sent = []

    def send(way, p, origin, cond=None):
        copy = shard_copy(way, p, origin, targets[way])
        sent.append((copy, cond))
        if cond is None:
            copy.start()
        else:
            pl.when(cond)(copy.start)

    def arrive(p, origin):
        shard_copy(0, p, origin, targets[0]).wait_recv()

    up, down = z < planes - 1, z > 0
    lines = [(y, x), (ya, xa)]
    far_lines = [(yb, xb), (1 - y, 1 - x)]

    def step(p, k):
        if k == 0:
            own[p].wait()
            mine = chip(y, z, x)
            for way, cond in ((1, up), (2, down), (0, None), (3, None), (4, None)):
                send(way, p, mine, cond)
            other = chip(ya, z, xa)
            arrive(p, other)
            for way, cond in ((1, up), (2, down), (3, None), (4, None)):
                send(way, p, other, cond)
            return
        for yy, xx in lines:
            for sign, way in ((-1, 1), (1, 2)):
                zz = z + sign * k
                valid = (zz >= 0) if sign < 0 else (zz < planes)
                onward = jnp.logical_and(valid, up if way == 1 else down)
                origin = chip(yy, zz, xx)
                pl.when(valid)(functools.partial(arrive, p, origin))
                send(way, p, origin, onward)
                send(3, p, origin, valid)
                send(4, p, origin, valid)

    def across(p, k):
        for yy, xx in far_lines:
            for sign in (-1, 1) if k else (0,):
                zz = z + sign * k
                valid = jnp.logical_and(zz >= 0, zz < planes)
                origin = chip(yy, zz, xx)
                pl.when(valid)(functools.partial(arrive, p, origin))
                send(4, p, origin, valid)

    def from_core(p):
        for origin in range(devices // CORES):
            pltpu.make_async_remote_copy(
                src_ref=wbuf.at[p, origin * CORES + 1 - core],
                dst_ref=wbuf.at[p, origin * CORES + 1 - core],
                send_sem=send_sem.at[4, p, origin],
                recv_sem=recv_sem.at[1, p, origin],
                device_id=targets[4],
                device_id_type=MESH,
            ).wait_recv()

    parts = 4 if devices % 4 == 0 else 1
    group = devices // parts
    span = group * rows

    def weights(p, i, low, high):
        block = wbuf[p, i * group : (i + 1) * group]
        return block.reshape(span, 2 * head)[:, low:high]

    def project(ref, p, low, high):
        total = None
        for i in range(parts):
            term = jnp.dot(
                ref[:, i * span : (i + 1) * span],
                weights(p, i, low, high),
                preferred_element_type=jnp.float32,
            )
            total = term if total is None else total + term
        return total

    place = x * CORES + core
    state_waits = []

    def plane_peer(j):
        return (x + j // 2) % 2, (core + j % 2) % 2

    def spread(e, local):
        st_send[e] = local.astype(jnp.bfloat16)
        for j in range(1, 4):
            px, pc = plane_peer(j)
            copy = pltpu.make_async_remote_copy(
                src_ref=st_send.at[e],
                dst_ref=st_in.at[e, place],
                send_sem=st_ss.at[e, j],
                recv_sem=st_rs.at[e, place],
                device_id=dev(y, z, px, pc),
                device_id_type=MESH,
            )
            copy.start()
            state_waits.append((copy, None))

    def plane_sum(e, local):
        total = local
        partial = jnp.zeros_like(local)
        for j in range(1, 4):
            px, pc = plane_peer(j)
            index = px * CORES + pc
            pltpu.make_async_remote_copy(
                src_ref=st_send.at[e],
                dst_ref=st_in.at[e, index],
                send_sem=st_ss.at[e, j],
                recv_sem=st_rs.at[e, index],
                device_id=dev(y, z, px, pc),
                device_id_type=MESH,
            ).wait_recv()
            block = st_in[e, index].astype(jnp.float32)
            total = total + block
            chosen = (index < place) if e == 0 else (index > place)
            partial = partial + jnp.where(chosen, block, 0.0)
        acc[...] = partial
        sum_send[e] = total.astype(jnp.bfloat16)
        for dz in range(1, planes):
            zz = z + dz if e == 0 else z - dz
            valid = (zz < planes) if e == 0 else (zz >= 0)
            copy = pltpu.make_async_remote_copy(
                src_ref=sum_send.at[e],
                dst_ref=sum_in.at[e, dz - 1],
                send_sem=sum_ss.at[e, dz - 1],
                recv_sem=sum_rs.at[e, dz - 1],
                device_id=dev(y, zz, x, core),
                device_id_type=MESH,
            )
            pl.when(valid)(copy.start)
            state_waits.append((copy, valid))

    def collect(e):
        for dz in range(1, planes):
            valid = (z - dz >= 0) if e == 0 else (z + dz < planes)

            @pl.when(valid)
            def _():
                pltpu.make_async_remote_copy(
                    src_ref=sum_send.at[e],
                    dst_ref=sum_in.at[e, dz - 1],
                    send_sem=sum_ss.at[e, dz - 1],
                    recv_sem=sum_rs.at[e, dz - 1],
                    device_id=targets[4],
                    device_id_type=MESH,
                ).wait_recv()
                acc[...] += sum_in[e, dz - 1].astype(jnp.float32)

        return acc[...].astype(jnp.bfloat16)

    for k in range(planes):
        step(0, k)
        if k >= 1:
            across(0, k - 1)
            step(1, k - 1)
        if k >= 2:
            across(1, k - 2)
    across(0, planes - 1)
    step(1, planes - 1)
    if planes >= 2:
        across(1, planes - 2)
    from_core(0)

    x_load.wait()
    kv = project(xv, 0, 0, 2 * head).astype(jnp.bfloat16)
    key_rows, value_rows = kv[:, :head], kv[:, head:]
    local_state = contract(key_rows, value_rows, 0, 0)
    spread(0, local_state)
    across(1, planes - 1)
    plane_sum(0, local_state)
    from_core(1)

    queries = project(xv, 1, 0, head).astype(jnp.bfloat16)
    g_load.wait()
    head_grad = project(gv, 1, head, 2 * head)
    row_ids = lax.broadcasted_iota(jnp.int32, (count, count), 0)
    col_ids = lax.broadcasted_iota(jnp.int32, (count, count), 1)
    causal = row_ids >= col_ids
    scores = jnp.where(causal, contract(queries, key_rows, 1, 1), 0.0).astype(jnp.bfloat16)
    intra_part = jnp.dot(scores, value_rows, preferred_element_type=jnp.float32)
    scaled = gain_ref[...] * head_grad
    prior_state = collect(0)
    attended = intra_part + jnp.dot(queries, prior_state, preferred_element_type=jnp.float32)
    inv_rms = lax.rsqrt(jnp.mean(attended * attended, axis=-1, keepdims=True) + 1e-06)
    attn_grad = inv_rms * scaled - attended * (inv_rms * inv_rms * inv_rms) * jnp.mean(
        attended * scaled, axis=-1, keepdims=True
    )
    attn_grad = attn_grad.astype(jnp.bfloat16)
    local_grad = contract(queries, attn_grad, 0, 0)
    spread(1, local_grad)
    prob_grad = jnp.where(causal, contract(attn_grad, value_rows, 1, 1), 0.0).astype(jnp.bfloat16)
    query_grad = jnp.dot(prob_grad, key_rows, preferred_element_type=jnp.float32) + contract(
        attn_grad, prior_state, 1, 1
    )
    query_grad = query_grad.astype(jnp.bfloat16)
    plane_sum(1, local_grad)
    key_part = contract(prob_grad, queries, 0, 0)
    value_part = contract(scores, attn_grad, 0, 0)
    later_state = collect(1)
    key_grad = key_part + contract(value_rows, later_state, 1, 1)
    value_grad = value_part + jnp.dot(key_rows, later_state, preferred_element_type=jnp.float32)
    joined = jnp.concatenate([key_grad, value_grad], axis=-1).astype(jnp.bfloat16)
    outs = []
    for i in range(parts):
        cols = pl.ds(i * span, span)
        ob[:, i * span : (i + 1) * span] = (
            contract(joined, weights(0, i, 0, 2 * head), 1, 1)
            + contract(query_grad, weights(1, i, 0, head), 1, 1)
        ).astype(jnp.bfloat16)
        copy = pltpu.make_async_copy(ob.at[:, cols], out_hbm.at[:, cols], out_sem.at[i])
        copy.start()
        outs.append(copy)
    for copy, cond in sent + state_waits:
        if cond is None:
            copy.wait_send()
        else:
            pl.when(cond)(copy.wait_send)
    for copy in outs:
        copy.wait()


def per_device_fused(devices, planes, inputs, w_project, w_output, norm_gain, out_grad):
    tokens, grads_in = inputs[0], out_grad[0]
    count, width = tokens.shape
    rows, _, head = w_project.shape
    keyval = w_project[:, 1:, :].reshape(rows, 2 * head)
    other = jnp.concatenate([w_project[:, 0, :], w_output], axis=-1)
    packed = jnp.stack([keyval, other])
    bf16, f32 = jnp.bfloat16, jnp.float32
    chips = devices // CORES
    hops = max(planes - 1, 1)
    dma = pltpu.SemaphoreType.DMA
    any_spec = pl.BlockSpec(memory_space=pl.ANY)
    result = pl.pallas_call(
        functools.partial(fused_kernel, planes),
        out_shape=jax.ShapeDtypeStruct((count, width), bf16),
        in_specs=[any_spec, any_spec, any_spec, pl.BlockSpec(memory_space=pltpu.VMEM)],
        out_specs=any_spec,
        scratch_shapes=[
            pltpu.VMEM((count, width), bf16),
            pltpu.VMEM((count, width), bf16),
            pltpu.VMEM((PIECES, devices, rows, 2 * head), bf16),
            pltpu.VMEM((count, width), bf16),
            pltpu.VMEM((2, head, head), bf16),
            pltpu.VMEM((2, 4, head, head), bf16),
            pltpu.VMEM((2, head, head), bf16),
            pltpu.VMEM((2, hops, head, head), bf16),
            pltpu.VMEM((head, head), f32),
            dma((2,)),
            dma((PIECES,)),
            dma((4,)),
            dma((2, PIECES, chips)),
            dma((5, PIECES, chips)),
            dma((2, 4)),
            dma((2, 4)),
            dma((2, hops)),
            dma((2, hops)),
        ],
        compiler_params=pltpu.CompilerParams(
            collective_id=0, has_side_effects=True, vmem_limit_bytes=48 * 1024 * 1024
        ),
    )(tokens, grads_in, packed, norm_gain.reshape(1, head))
    return result[None]


def per_device(ndp, nseq, inputs, w_project, w_output, norm_gain, out_grad):
    rows, head = w_project.shape[0], w_project.shape[2]
    fits = (
        ndp == 2
        and nseq % (CORES * WIDE) == 0
        and inputs.shape[0] == 1
        and rows % 16 == 0
        and (ndp * nseq // 4 * rows) % 128 == 0
        and head % 128 == 0
    )
    if not fits:
        return per_device_plain(inputs, w_project, w_output, norm_gain, out_grad)
    return per_device_fused(
        ndp * nseq, nseq // (CORES * WIDE), inputs, w_project, w_output, norm_gain, out_grad
    )


def solution(mesh):
    in_specs = (
        P("dp", "seq", None),
        P(("dp", "seq"), None, None),
        P(("dp", "seq"), None),
        P(),
        P("dp", "seq", None),
    )
    out_specs = P("dp", "seq", None)
    return jax.shard_map(
        functools.partial(per_device, mesh.shape["dp"], mesh.shape["seq"]),
        mesh=mesh, in_specs=in_specs, out_specs=out_specs, check_vma=False
    )
```

```python
import functools

import jax
import jax.numpy as jnp
from jax import lax
from jax.experimental import pallas as pl
from jax.experimental.pallas import tpu as pltpu
from jax.sharding import PartitionSpec as P


def contract(left, right, left_dim, right_dim):
    return lax.dot_general(
        left, right, (((left_dim,), (right_dim,)), ((), ())), preferred_element_type=jnp.float32
    )


def other_blocks(local, reverse):
    every = lax.all_gather(local[None].astype(jnp.bfloat16), "seq", axis=0, tiled=True).astype(
        jnp.float32
    )
    own_index = lax.axis_index("seq")
    rank_list = jnp.arange(every.shape[0], dtype=jnp.int32)
    if reverse:
        selected = rank_list > own_index
    else:
        selected = rank_list < own_index
    return jnp.sum(jnp.where(selected[:, None, None], every, 0.0), axis=0)


def per_device_plain(inputs, w_project, w_output, norm_gain, out_grad):
    proj_full, out_full = (
        lax.all_gather(w_project, ("dp", "seq"), axis=0, tiled=True),
        lax.all_gather(w_output, ("dp", "seq"), axis=0, tiled=True),
    )
    width = proj_full.shape[0]
    head = proj_full.shape[2]
    flat_proj = proj_full.reshape(width, 3 * head)
    tokens = inputs[0]
    grads_in = out_grad[0]
    count = tokens.shape[0]
    projected = jnp.dot(tokens, flat_proj, preferred_element_type=jnp.float32).astype(jnp.bfloat16)
    queries = projected[:, :head]
    key_rows = projected[:, head : 2 * head]
    value_rows = projected[:, 2 * head :]
    row_ids = lax.broadcasted_iota(jnp.int32, (count, count), 0)
    col_ids = lax.broadcasted_iota(jnp.int32, (count, count), 1)
    causal = row_ids >= col_ids
    scores = jnp.where(causal, contract(queries, key_rows, 1, 1), 0.0).astype(jnp.bfloat16)
    intra_part = jnp.dot(scores, value_rows, preferred_element_type=jnp.float32)
    local_state = contract(key_rows, value_rows, 0, 0)
    prior_state = other_blocks(local_state, False).astype(jnp.bfloat16)
    attended = intra_part + jnp.dot(queries, prior_state, preferred_element_type=jnp.float32)
    inv_rms = lax.rsqrt(jnp.mean(attended * attended, axis=-1, keepdims=True) + 1e-06)
    head_grad = jnp.dot(grads_in, out_full, preferred_element_type=jnp.float32)
    scaled = norm_gain * head_grad
    attn_grad = inv_rms * scaled - attended * inv_rms**3 * jnp.mean(
        attended * scaled, axis=-1, keepdims=True
    )
    attn_grad = attn_grad.astype(jnp.bfloat16)
    prob_grad = jnp.where(causal, contract(attn_grad, value_rows, 1, 1), 0.0).astype(jnp.bfloat16)
    local_grad = contract(queries, attn_grad, 0, 0)
    later_state = other_blocks(local_grad, True).astype(jnp.bfloat16)
    query_grad = jnp.dot(prob_grad, key_rows, preferred_element_type=jnp.float32) + contract(
        attn_grad, prior_state, 1, 1
    )
    key_grad = contract(prob_grad, queries, 0, 0) + contract(value_rows, later_state, 1, 1)
    value_grad = contract(scores, attn_grad, 0, 0) + jnp.dot(
        key_rows, later_state, preferred_element_type=jnp.float32
    )
    joined = jnp.concatenate([query_grad, key_grad, value_grad], axis=-1).astype(jnp.bfloat16)
    result = contract(joined, flat_proj, 1, 1).astype(jnp.bfloat16)
    return result[None]


CORES = 2
WIDE = 2
PIECES = 2
MESH = pl.DeviceIdType.MESH
FIRST, UP, DOWN, LAST, CORE = range(5)


def fused_kernel(
    planes, x_hbm, g_hbm, w_hbm, o_hbm, gain_ref, out_hbm,
    xv, gv, wbuf, ob, proj, query_out, st_send, st_in, sum_send, sum_in, acc,
    load_sem, own_sem, out_sem, recv_sem, send_sem, st_rs, st_ss, sum_rs, sum_ss,
):
    y = lax.axis_index("dp")
    seq = lax.axis_index("seq")
    core = seq % CORES
    x = (seq // CORES) % WIDE
    z = seq // (CORES * WIDE)
    head = st_send.shape[-1]
    count, width = xv.shape
    devices = wbuf.shape[1]
    rows = wbuf.shape[2]
    ya, xa = (y + core) % 2, (x + 1 - core) % 2
    yb, xb = (y + 1 - core) % 2, (x + core) % 2

    def dev(yy, zz, xx, cc):
        return (yy, (zz * WIDE + xx) * CORES + cc)

    def chip(yy, zz, xx):
        return (yy * planes + zz) * WIDE + xx

    x_load = pltpu.make_async_copy(x_hbm, xv, load_sem.at[0])
    g_load = pltpu.make_async_copy(g_hbm, gv, load_sem.at[1])
    me = chip(y, z, x) * CORES + core
    own = [
        [
            pltpu.make_async_copy(
                w_hbm.at[1 + j], wbuf.at[0, me, :, pl.ds(j * head, head)], own_sem.at[3 * j]
            )
            for j in range(2)
        ],
        [
            pltpu.make_async_copy(
                w_hbm.at[0], wbuf.at[1, me, :, pl.ds(0, head)], own_sem.at[1]
            ),
            pltpu.make_async_copy(o_hbm, wbuf.at[1, me, :, pl.ds(head, head)], own_sem.at[2]),
        ],
    ]
    for copies in own:
        for copy in copies:
            copy.start()
    x_load.start()
    g_load.start()

    barrier = pltpu.get_barrier_semaphore()
    near = [
        dev(y, z, x, 1 - core),
        dev(y, z, 1 - x, core),
        dev(y, z, 1 - x, 1 - core),
        dev(1 - y, z, x, core),
    ] + [dev(y, (z + dz) % planes, x, core) for dz in range(1, planes)]
    for other in near:
        pl.semaphore_signal(barrier, inc=1, device_id=other, device_id_type=MESH)
    pl.semaphore_wait(barrier, len(near))

    cut = rows * 2 // 3 // 16 * 16
    spans = (pl.ds(0, cut), pl.ds(cut, rows - cut))

    def shard_copy(way, p, part, origin, owner, target):
        slot = wbuf.at[p, origin * CORES + owner, spans[part]]
        return pltpu.make_async_remote_copy(
            src_ref=slot,
            dst_ref=slot,
            send_sem=send_sem.at[way, p, part, origin],
            recv_sem=recv_sem.at[1 if way == CORE else 0, p, part, origin],
            device_id=target,
            device_id_type=MESH,
        )

    targets = [
        dev(ya, z, xa, core),
        dev(y, lax.rem(z + 1, planes), x, core),
        dev(y, lax.rem(z + planes - 1, planes), x, core),
        dev(yb, z, xb, core),
        dev(y, z, x, 1 - core),
    ]
    sent = []

    def send(way, p, part, origin, cond=None):
        copy = shard_copy(way, p, part, origin, core, targets[way])
        sent.append((copy, cond))
        if cond is None:
            copy.start()
        else:
            pl.when(cond)(copy.start)

    def arrive(p, part, origin, valid=None):
        wait = shard_copy(FIRST, p, part, origin, core, targets[FIRST]).wait_recv
        if valid is None:
            wait()
        else:
            pl.when(valid)(wait)

    up, down = z < planes - 1, z > 0

    def both_ways(k):
        if k == 0:
            return [(z, None, None)]
        return [(z - k, z - k >= 0, 1), (z + k, z + k < planes, -1)]

    def begin(p):
        for copy in own[p]:
            copy.wait()
        mine = chip(y, z, x)
        for part in range(2):
            send(UP, p, part, mine, up)
            send(DOWN, p, part, mine, down)
            send(FIRST, p, part, mine)
        for part in range(2):
            send(LAST, p, part, mine)
            send(CORE, p, part, mine)

    def step(p, k):
        if k == 0:
            other = chip(ya, z, xa)
            arrive(p, 0, other)
            send(UP, p, 0, other, up)
            send(DOWN, p, 0, other, down)
            send(LAST, p, 0, other)
            send(CORE, p, 0, other)
            return
        for part, (yy, xx) in ((0, (y, x)), (1, (y, x)), (0, (ya, xa))):
            for zz, valid, sign in both_ways(k):
                origin = chip(yy, zz, xx)
                arrive(p, part, origin, valid)
                if sign == 1:
                    send(UP, p, part, origin, jnp.logical_and(valid, up))
                else:
                    send(DOWN, p, part, origin, jnp.logical_and(valid, down))
                if part == 1:
                    send(FIRST, p, part, origin, valid)
                send(LAST, p, part, origin, valid)
                send(CORE, p, part, origin, valid)

    def across(p, k):
        for zz, valid, _ in both_ways(k):
            origin = chip(ya, zz, xa)
            arrive(p, 1, origin, valid)
            send(LAST, p, 1, origin, valid)
            send(CORE, p, 1, origin, valid)
        for part, (yy, xx) in ((0, (yb, xb)), (1, (yb, xb)), (0, (1 - y, 1 - x))):
            for zz, valid, _ in both_ways(k):
                origin = chip(yy, zz, xx)
                arrive(p, part, origin, valid)
                send(CORE, p, part, origin, valid)

    def settle(p, k):
        for zz, valid, _ in both_ways(k):
            origin = chip(1 - y, zz, 1 - x)
            arrive(p, 1, origin, valid)
            send(CORE, p, 1, origin, valid)
        for zz, valid, _ in both_ways(k):

            def finish():
                for yy in range(2):
                    for xx in range(WIDE):
                        for part in range(2):
                            shard_copy(
                                CORE, p, part, chip(yy, zz, xx), 1 - core, targets[CORE]
                            ).wait_recv()
                project(p, zz, k == 0)

            if valid is None:
                finish()
            else:
                pl.when(valid)(finish)

    def project(p, zz, first):
        if first:
            (x_load, g_load)[p].wait()
        terms = []
        for yy in range(2):
            base = (yy * planes + zz) * WIDE * CORES
            cols = pl.ds(pl.multiple_of(base * rows, 128), WIDE * CORES * rows)
            block = wbuf[p, pl.ds(base, WIDE * CORES)].reshape(WIDE * CORES * rows, 2 * head)
            if p == 0:
                terms.append(jnp.dot(xv[:, cols], block, preferred_element_type=jnp.float32))
            else:
                terms.append(
                    jnp.concatenate(
                        [
                            jnp.dot(
                                xv[:, cols], block[:, :head], preferred_element_type=jnp.float32
                            ),
                            jnp.dot(
                                gv[:, cols], block[:, head:], preferred_element_type=jnp.float32
                            ),
                        ],
                        axis=-1,
                    )
                )
        total = terms[0] + terms[1]
        proj[p] = total if first else proj[p] + total

    parts = 4 if devices % 4 == 0 else 1
    group = devices // parts
    span = group * rows

    def weights(p, i, low, high):
        block = wbuf[p, i * group : (i + 1) * group]
        return block.reshape(span, 2 * head)[:, low:high]

    place = x * CORES + core
    state_waits = []

    def plane_peer(j):
        return (x + j // 2) % 2, (core + j % 2) % 2

    def spread(e, local):
        st_send[e] = local.astype(jnp.bfloat16)
        for j in range(1, 4):
            px, pc = plane_peer(j)
            copy = pltpu.make_async_remote_copy(
                src_ref=st_send.at[e],
                dst_ref=st_in.at[e, place],
                send_sem=st_ss.at[e, j],
                recv_sem=st_rs.at[e, place],
                device_id=dev(y, z, px, pc),
                device_id_type=MESH,
            )
            copy.start()
            state_waits.append((copy, None))

    def plane_sum(e, local):
        total = local
        partial = jnp.zeros_like(local)
        for j in range(1, 4):
            px, pc = plane_peer(j)
            index = px * CORES + pc
            pltpu.make_async_remote_copy(
                src_ref=st_send.at[e],
                dst_ref=st_in.at[e, index],
                send_sem=st_ss.at[e, j],
                recv_sem=st_rs.at[e, index],
                device_id=dev(y, z, px, pc),
                device_id_type=MESH,
            ).wait_recv()
            block = st_in[e, index].astype(jnp.float32)
            total = total + block
            chosen = (index < place) if e == 0 else (index > place)
            partial = partial + jnp.where(chosen, block, 0.0)
        acc[...] = partial
        sum_send[e] = total.astype(jnp.bfloat16)
        for dz in range(1, planes):
            zz = z + dz if e == 0 else z - dz
            valid = (zz < planes) if e == 0 else (zz >= 0)
            copy = pltpu.make_async_remote_copy(
                src_ref=sum_send.at[e],
                dst_ref=sum_in.at[e, dz - 1],
                send_sem=sum_ss.at[e, dz - 1],
                recv_sem=sum_rs.at[e, dz - 1],
                device_id=dev(y, zz, x, core),
                device_id_type=MESH,
            )
            pl.when(valid)(copy.start)
            state_waits.append((copy, valid))

    def collect(e):
        for dz in range(1, planes):
            valid = (z - dz >= 0) if e == 0 else (z + dz < planes)

            @pl.when(valid)
            def _():
                pltpu.make_async_remote_copy(
                    src_ref=sum_send.at[e],
                    dst_ref=sum_in.at[e, dz - 1],
                    send_sem=sum_ss.at[e, dz - 1],
                    recv_sem=sum_rs.at[e, dz - 1],
                    device_id=targets[CORE],
                    device_id_type=MESH,
                ).wait_recv()
                acc[...] += sum_in[e, dz - 1].astype(jnp.float32)

        return acc[...].astype(jnp.bfloat16)

    for p in range(PIECES):
        begin(p)
    order = [(p, k) for k in range(planes) for p in range(PIECES)]
    keyval_at = order.index((0, planes - 1)) + 2
    for i in range(len(order) + 2):
        if i < len(order):
            step(*order[i])
        if 1 <= i <= len(order):
            across(*order[i - 1])
        if i == keyval_at + 1:
            plane_sum(0, local_state)
        if i >= 2:
            settle(*order[i - 2])
        if i == keyval_at:
            kv = proj[0].astype(jnp.bfloat16)
            key_rows, value_rows = kv[:, :head], kv[:, head:]
            local_state = contract(key_rows, value_rows, 0, 0)
            spread(0, local_state)

    queries = proj[1, :, :head].astype(jnp.bfloat16)
    head_grad = proj[1, :, head:]
    row_ids = lax.broadcasted_iota(jnp.int32, (count, count), 0)
    col_ids = lax.broadcasted_iota(jnp.int32, (count, count), 1)
    causal = row_ids >= col_ids
    scores = jnp.where(causal, contract(queries, key_rows, 1, 1), 0.0).astype(jnp.bfloat16)
    intra_part = jnp.dot(scores, value_rows, preferred_element_type=jnp.float32)
    scaled = gain_ref[...] * head_grad
    prior_state = collect(0)
    attended = intra_part + jnp.dot(queries, prior_state, preferred_element_type=jnp.float32)
    inv_rms = lax.rsqrt(jnp.mean(attended * attended, axis=-1, keepdims=True) + 1e-06)
    attn_grad = inv_rms * scaled - attended * (inv_rms * inv_rms * inv_rms) * jnp.mean(
        attended * scaled, axis=-1, keepdims=True
    )
    attn_grad = attn_grad.astype(jnp.bfloat16)
    local_grad = contract(queries, attn_grad, 0, 0)
    spread(1, local_grad)
    prob_grad = jnp.where(causal, contract(attn_grad, value_rows, 1, 1), 0.0).astype(jnp.bfloat16)
    query_grad = jnp.dot(prob_grad, key_rows, preferred_element_type=jnp.float32) + contract(
        attn_grad, prior_state, 1, 1
    )
    query_grad = query_grad.astype(jnp.bfloat16)
    plane_sum(1, local_grad)
    key_part = contract(prob_grad, queries, 0, 0)
    value_part = contract(scores, attn_grad, 0, 0)
    for i in range(parts):
        query_out[:, i * span : (i + 1) * span] = contract(
            query_grad, weights(1, i, 0, head), 1, 1
        )
    later_state = collect(1)
    key_grad = key_part + contract(value_rows, later_state, 1, 1)
    value_grad = value_part + jnp.dot(key_rows, later_state, preferred_element_type=jnp.float32)
    joined = jnp.concatenate([key_grad, value_grad], axis=-1).astype(jnp.bfloat16)
    outs = []
    for i in range(parts):
        cols = pl.ds(i * span, span)
        ob[:, i * span : (i + 1) * span] = (
            contract(joined, weights(0, i, 0, 2 * head), 1, 1)
            + query_out[:, i * span : (i + 1) * span]
        ).astype(jnp.bfloat16)
        copy = pltpu.make_async_copy(ob.at[:, cols], out_hbm.at[:, cols], out_sem.at[i])
        copy.start()
        outs.append(copy)
    for copy, cond in sent + state_waits:
        if cond is None:
            copy.wait_send()
        else:
            pl.when(cond)(copy.wait_send)
    for copy in outs:
        copy.wait()


def per_device_fused(devices, planes, inputs, w_project, w_output, norm_gain, out_grad):
    tokens, grads_in = inputs[0], out_grad[0]
    count, width = tokens.shape
    rows, _, head = w_project.shape
    bf16, f32 = jnp.bfloat16, jnp.float32
    chips = devices // CORES
    hops = max(planes - 1, 1)
    dma = pltpu.SemaphoreType.DMA
    any_spec = pl.BlockSpec(memory_space=pl.ANY)
    result = pl.pallas_call(
        functools.partial(fused_kernel, planes),
        out_shape=jax.ShapeDtypeStruct((count, width), bf16),
        in_specs=[pl.BlockSpec(memory_space=pltpu.HBM)] * 4 + [pl.BlockSpec(memory_space=pltpu.VMEM)],
        out_specs=any_spec,
        scratch_shapes=[
            pltpu.VMEM((count, width), bf16),
            pltpu.VMEM((count, width), bf16),
            pltpu.VMEM((PIECES, devices, rows, 2 * head), bf16),
            pltpu.VMEM((count, width), bf16),
            pltpu.VMEM((PIECES, count, 2 * head), f32),
            pltpu.VMEM((count, width), f32),
            pltpu.VMEM((2, head, head), bf16),
            pltpu.VMEM((2, 4, head, head), bf16),
            pltpu.VMEM((2, head, head), bf16),
            pltpu.VMEM((2, hops, head, head), bf16),
            pltpu.VMEM((head, head), f32),
            dma((2,)),
            dma((4,)),
            dma((4,)),
            dma((2, PIECES, 2, chips)),
            dma((5, PIECES, 2, chips)),
            dma((2, 4)),
            dma((2, 4)),
            dma((2, hops)),
            dma((2, hops)),
        ],
        compiler_params=pltpu.CompilerParams(
            collective_id=0, has_side_effects=True, vmem_limit_bytes=67043328
        ),
    )(tokens, grads_in, jnp.transpose(w_project, (1, 0, 2)), w_output, norm_gain.reshape(1, head))
    return result[None]


def per_device(ndp, nseq, inputs, w_project, w_output, norm_gain, out_grad):
    rows, head = w_project.shape[0], w_project.shape[2]
    fits = (
        ndp == 2
        and nseq % (CORES * WIDE) == 0
        and inputs.shape[0] == 1
        and rows % 16 == 0
        and (ndp * nseq // 4 * rows) % 128 == 0
        and head % 128 == 0
    )
    if not fits:
        return per_device_plain(inputs, w_project, w_output, norm_gain, out_grad)
    return per_device_fused(
        ndp * nseq, nseq // (CORES * WIDE), inputs, w_project, w_output, norm_gain, out_grad
    )


def solution(mesh):
    in_specs = (
        P("dp", "seq", None),
        P(("dp", "seq"), None, None),
        P(("dp", "seq"), None),
        P(),
        P("dp", "seq", None),
    )
    out_specs = P("dp", "seq", None)
    return jax.shard_map(
        functools.partial(per_device, mesh.shape["dp"], mesh.shape["seq"]),
        mesh=mesh, in_specs=in_specs, out_specs=out_specs, check_vma=False
    )
```

```python
import functools

import jax
import jax.numpy as jnp
from jax import lax
from jax.experimental import pallas as pl
from jax.experimental.pallas import tpu as pltpu
from jax.sharding import PartitionSpec as P


def contract(left, right, left_dim, right_dim):
    return lax.dot_general(
        left, right, (((left_dim,), (right_dim,)), ((), ())), preferred_element_type=jnp.float32
    )


def other_blocks(local, reverse):
    every = lax.all_gather(local[None].astype(jnp.bfloat16), "seq", axis=0, tiled=True).astype(
        jnp.float32
    )
    own_index = lax.axis_index("seq")
    rank_list = jnp.arange(every.shape[0], dtype=jnp.int32)
    if reverse:
        selected = rank_list > own_index
    else:
        selected = rank_list < own_index
    return jnp.sum(jnp.where(selected[:, None, None], every, 0.0), axis=0)


def per_device_plain(inputs, w_project, w_output, norm_gain, out_grad):
    proj_full, out_full = (
        lax.all_gather(w_project, ("dp", "seq"), axis=0, tiled=True),
        lax.all_gather(w_output, ("dp", "seq"), axis=0, tiled=True),
    )
    width = proj_full.shape[0]
    head = proj_full.shape[2]
    flat_proj = proj_full.reshape(width, 3 * head)
    tokens = inputs[0]
    grads_in = out_grad[0]
    count = tokens.shape[0]
    projected = jnp.dot(tokens, flat_proj, preferred_element_type=jnp.float32).astype(jnp.bfloat16)
    queries = projected[:, :head]
    key_rows = projected[:, head : 2 * head]
    value_rows = projected[:, 2 * head :]
    row_ids = lax.broadcasted_iota(jnp.int32, (count, count), 0)
    col_ids = lax.broadcasted_iota(jnp.int32, (count, count), 1)
    causal = row_ids >= col_ids
    scores = jnp.where(causal, contract(queries, key_rows, 1, 1), 0.0).astype(jnp.bfloat16)
    intra_part = jnp.dot(scores, value_rows, preferred_element_type=jnp.float32)
    local_state = contract(key_rows, value_rows, 0, 0)
    prior_state = other_blocks(local_state, False).astype(jnp.bfloat16)
    attended = intra_part + jnp.dot(queries, prior_state, preferred_element_type=jnp.float32)
    inv_rms = lax.rsqrt(jnp.mean(attended * attended, axis=-1, keepdims=True) + 1e-06)
    head_grad = jnp.dot(grads_in, out_full, preferred_element_type=jnp.float32)
    scaled = norm_gain * head_grad
    attn_grad = inv_rms * scaled - attended * inv_rms**3 * jnp.mean(
        attended * scaled, axis=-1, keepdims=True
    )
    attn_grad = attn_grad.astype(jnp.bfloat16)
    prob_grad = jnp.where(causal, contract(attn_grad, value_rows, 1, 1), 0.0).astype(jnp.bfloat16)
    local_grad = contract(queries, attn_grad, 0, 0)
    later_state = other_blocks(local_grad, True).astype(jnp.bfloat16)
    query_grad = jnp.dot(prob_grad, key_rows, preferred_element_type=jnp.float32) + contract(
        attn_grad, prior_state, 1, 1
    )
    key_grad = contract(prob_grad, queries, 0, 0) + contract(value_rows, later_state, 1, 1)
    value_grad = contract(scores, attn_grad, 0, 0) + jnp.dot(
        key_rows, later_state, preferred_element_type=jnp.float32
    )
    joined = jnp.concatenate([query_grad, key_grad, value_grad], axis=-1).astype(jnp.bfloat16)
    result = contract(joined, flat_proj, 1, 1).astype(jnp.bfloat16)
    return result[None]


CORES = 2
WIDE = 2
PIECES = 2
ROUTED = 1
PARTS = 1
MESH = pl.DeviceIdType.MESH
FIRST, UP, DOWN, LAST, CORE = range(5)


def fused_kernel(
    planes, x_hbm, g_hbm, w_hbm, o_hbm, gain_ref, out_hbm,
    xv, gv, wbuf, ob, proj, query_out, st_send, st_in, sum_send, sum_in, acc,
    load_sem, own_sem, out_sem, recv_sem, send_sem, st_rs, st_ss, sum_rs, sum_ss,
):
    y = lax.axis_index("dp")
    seq = lax.axis_index("seq")
    core = seq % CORES
    x = (seq // CORES) % WIDE
    z = seq // (CORES * WIDE)
    head = st_send.shape[-1]
    count, width = xv.shape
    devices = wbuf.shape[1]
    rows = wbuf.shape[2]
    ya, xa = (y + core) % 2, (x + 1 - core) % 2
    yb, xb = (y + 1 - core) % 2, (x + core) % 2

    def dev(yy, zz, xx, cc):
        return (yy, (zz * WIDE + xx) * CORES + cc)

    def chip(yy, zz, xx):
        return (yy * planes + zz) * WIDE + xx

    x_load = pltpu.make_async_copy(x_hbm, xv, load_sem.at[0])
    g_load = pltpu.make_async_copy(g_hbm, gv, load_sem.at[1])
    me = chip(y, z, x) * CORES + core
    own = [
        [
            pltpu.make_async_copy(
                w_hbm.at[1 + j], wbuf.at[0, me, :, pl.ds(j * head, head)], own_sem.at[3 * j]
            )
            for j in range(2)
        ],
        [
            pltpu.make_async_copy(
                w_hbm.at[0], wbuf.at[1, me, :, pl.ds(0, head)], own_sem.at[1]
            ),
            pltpu.make_async_copy(o_hbm, wbuf.at[1, me, :, pl.ds(head, head)], own_sem.at[2]),
        ],
    ]
    for copies in own:
        for copy in copies:
            copy.start()
    x_load.start()
    g_load.start()

    barrier = pltpu.get_barrier_semaphore()
    near = [
        dev(y, z, x, 1 - core),
        dev(y, z, 1 - x, core),
        dev(y, z, 1 - x, 1 - core),
        dev(1 - y, z, x, core),
    ] + [dev(y, (z + dz) % planes, x, core) for dz in range(1, planes)]
    for other in near:
        pl.semaphore_signal(barrier, inc=1, device_id=other, device_id_type=MESH)
    pl.semaphore_wait(barrier, len(near))

    spans = (pl.ds(0, rows),)

    def shard_copy(way, p, part, origin, owner, target):
        slot = wbuf.at[p, origin * CORES + owner, spans[part]]
        return pltpu.make_async_remote_copy(
            src_ref=slot,
            dst_ref=slot,
            send_sem=send_sem.at[way, p, part, origin],
            recv_sem=recv_sem.at[1 if way == CORE else 0, p, part, origin],
            device_id=target,
            device_id_type=MESH,
        )

    targets = [
        dev(ya, z, xa, core),
        dev(y, lax.rem(z + 1, planes), x, core),
        dev(y, lax.rem(z + planes - 1, planes), x, core),
        dev(yb, z, xb, core),
        dev(y, z, x, 1 - core),
    ]
    sent = []

    def send(way, p, part, origin, cond=None):
        copy = shard_copy(way, p, part, origin, core, targets[way])
        sent.append((copy, cond))
        if cond is None:
            copy.start()
        else:
            pl.when(cond)(copy.start)

    def arrive(p, part, origin, valid=None):
        wait = shard_copy(FIRST, p, part, origin, core, targets[FIRST]).wait_recv
        if valid is None:
            wait()
        else:
            pl.when(valid)(wait)

    up, down = z < planes - 1, z > 0

    def both_ways(k):
        if k == 0:
            return [(z, None, None)]
        return [(z - k, z - k >= 0, 1), (z + k, z + k < planes, -1)]

    def begin(p):
        for copy in own[p]:
            copy.wait()
        mine = chip(y, z, x)
        for part in range(PARTS):
            send(UP, p, part, mine, up)
            send(DOWN, p, part, mine, down)
            send(FIRST, p, part, mine)
        for part in range(PARTS):
            send(LAST, p, part, mine)
            send(CORE, p, part, mine)

    def step(p, k):
        if k == 0:
            other = chip(ya, z, xa)
            for part in range(ROUTED):
                arrive(p, part, other)
                send(UP, p, part, other, up)
                send(DOWN, p, part, other, down)
                send(LAST, p, part, other)
                send(CORE, p, part, other)
            return
        for part, (yy, xx) in [(part, (y, x)) for part in range(PARTS)] + [
            (part, (ya, xa)) for part in range(ROUTED)
        ]:
            for zz, valid, sign in both_ways(k):
                origin = chip(yy, zz, xx)
                arrive(p, part, origin, valid)
                if sign == 1:
                    send(UP, p, part, origin, jnp.logical_and(valid, up))
                else:
                    send(DOWN, p, part, origin, jnp.logical_and(valid, down))
                if part >= ROUTED:
                    send(FIRST, p, part, origin, valid)
                send(LAST, p, part, origin, valid)
                send(CORE, p, part, origin, valid)

    def across(p, k):
        for part, (yy, xx) in [(part, (yb, xb)) for part in range(PARTS)] + [
            (part, (1 - y, 1 - x)) for part in range(ROUTED)
        ]:
            for zz, valid, _ in both_ways(k):
                origin = chip(yy, zz, xx)
                arrive(p, part, origin, valid)
                send(CORE, p, part, origin, valid)

    def settle(p, k):
        for zz, valid, _ in both_ways(k):

            def finish():
                for yy in range(2):
                    for xx in range(WIDE):
                        for part in range(PARTS):
                            shard_copy(
                                CORE, p, part, chip(yy, zz, xx), 1 - core, targets[CORE]
                            ).wait_recv()
                project(p, zz, k == 0)

            if valid is None:
                finish()
            else:
                pl.when(valid)(finish)

    def project(p, zz, first):
        if first:
            (x_load, g_load)[p].wait()
        terms = []
        for yy in range(2):
            base = (yy * planes + zz) * WIDE * CORES
            cols = pl.ds(pl.multiple_of(base * rows, 128), WIDE * CORES * rows)
            block = wbuf[p, pl.ds(base, WIDE * CORES)].reshape(WIDE * CORES * rows, 2 * head)
            if p == 0:
                terms.append(jnp.dot(xv[:, cols], block, preferred_element_type=jnp.float32))
            else:
                terms.append(
                    jnp.concatenate(
                        [
                            jnp.dot(
                                xv[:, cols], block[:, :head], preferred_element_type=jnp.float32
                            ),
                            jnp.dot(
                                gv[:, cols], block[:, head:], preferred_element_type=jnp.float32
                            ),
                        ],
                        axis=-1,
                    )
                )
        total = terms[0] + terms[1]
        proj[p] = total if first else proj[p] + total

    parts = 4 if devices % 4 == 0 else 1
    group = devices // parts
    span = group * rows

    def weights(p, i, low, high):
        block = wbuf[p, i * group : (i + 1) * group]
        return block.reshape(span, 2 * head)[:, low:high]

    place = x * CORES + core
    state_waits = []

    def plane_peer(j):
        return (x + j // 2) % 2, (core + j % 2) % 2

    def spread(e, local):
        st_send[e] = local.astype(jnp.bfloat16)
        for j in (2, 3, 1):
            px, pc = plane_peer(j)
            copy = pltpu.make_async_remote_copy(
                src_ref=st_send.at[e],
                dst_ref=st_in.at[e, place],
                send_sem=st_ss.at[e, j],
                recv_sem=st_rs.at[e, place],
                device_id=dev(y, z, px, pc),
                device_id_type=MESH,
            )
            copy.start()
            state_waits.append((copy, None))

    def plane_sum(e, local):
        total = local
        partial = jnp.zeros_like(local)
        for j in range(1, 4):
            px, pc = plane_peer(j)
            index = px * CORES + pc
            pltpu.make_async_remote_copy(
                src_ref=st_send.at[e],
                dst_ref=st_in.at[e, index],
                send_sem=st_ss.at[e, j],
                recv_sem=st_rs.at[e, index],
                device_id=dev(y, z, px, pc),
                device_id_type=MESH,
            ).wait_recv()
            block = st_in[e, index].astype(jnp.float32)
            total = total + block
            chosen = (index < place) if e == 0 else (index > place)
            partial = partial + jnp.where(chosen, block, 0.0)
        acc[...] = partial
        sum_send[e] = total.astype(jnp.bfloat16)
        for dz in range(planes - 1, 0, -1):
            zz = z + dz if e == 0 else z - dz
            valid = (zz < planes) if e == 0 else (zz >= 0)
            copy = pltpu.make_async_remote_copy(
                src_ref=sum_send.at[e],
                dst_ref=sum_in.at[e, dz - 1],
                send_sem=sum_ss.at[e, dz - 1],
                recv_sem=sum_rs.at[e, dz - 1],
                device_id=dev(y, zz, x, core),
                device_id_type=MESH,
            )
            pl.when(valid)(copy.start)
            state_waits.append((copy, valid))

    def collect(e):
        for dz in range(1, planes):
            valid = (z - dz >= 0) if e == 0 else (z + dz < planes)

            @pl.when(valid)
            def _():
                pltpu.make_async_remote_copy(
                    src_ref=sum_send.at[e],
                    dst_ref=sum_in.at[e, dz - 1],
                    send_sem=sum_ss.at[e, dz - 1],
                    recv_sem=sum_rs.at[e, dz - 1],
                    device_id=targets[CORE],
                    device_id_type=MESH,
                ).wait_recv()
                acc[...] += sum_in[e, dz - 1].astype(jnp.float32)

        return acc[...].astype(jnp.bfloat16)

    for p in range(PIECES):
        begin(p)
    order = [(p, k) for k in range(planes) for p in range(PIECES)]
    keyval_at = order.index((0, planes - 1)) + 2
    for i in range(len(order) + 2):
        if i < len(order):
            step(*order[i])
        if 1 <= i <= len(order):
            across(*order[i - 1])
        if i == keyval_at + 1:
            plane_sum(0, local_state)
        if i >= 2:
            settle(*order[i - 2])
        if i == keyval_at:
            kv = proj[0].astype(jnp.bfloat16)
            key_rows, value_rows = kv[:, :head], kv[:, head:]
            local_state = contract(key_rows, value_rows, 0, 0)
            spread(0, local_state)

    queries = proj[1, :, :head].astype(jnp.bfloat16)
    head_grad = proj[1, :, head:]
    row_ids = lax.broadcasted_iota(jnp.int32, (count, count), 0)
    col_ids = lax.broadcasted_iota(jnp.int32, (count, count), 1)
    causal = row_ids >= col_ids
    scores = jnp.where(causal, contract(queries, key_rows, 1, 1), 0.0).astype(jnp.bfloat16)
    intra_part = jnp.dot(scores, value_rows, preferred_element_type=jnp.float32)
    scaled = gain_ref[...] * head_grad
    prior_state = collect(0)
    attended = intra_part + jnp.dot(queries, prior_state, preferred_element_type=jnp.float32)
    inv_rms = lax.rsqrt(jnp.mean(attended * attended, axis=-1, keepdims=True) + 1e-06)
    attn_grad = inv_rms * scaled - attended * (inv_rms * inv_rms * inv_rms) * jnp.mean(
        attended * scaled, axis=-1, keepdims=True
    )
    attn_grad = attn_grad.astype(jnp.bfloat16)
    local_grad = contract(queries, attn_grad, 0, 0)
    spread(1, local_grad)
    prob_grad = jnp.where(causal, contract(attn_grad, value_rows, 1, 1), 0.0).astype(jnp.bfloat16)
    query_grad = jnp.dot(prob_grad, key_rows, preferred_element_type=jnp.float32) + contract(
        attn_grad, prior_state, 1, 1
    )
    query_grad = query_grad.astype(jnp.bfloat16)
    plane_sum(1, local_grad)
    key_part = contract(prob_grad, queries, 0, 0)
    value_part = contract(scores, attn_grad, 0, 0)
    for i in range(parts):
        query_out[:, i * span : (i + 1) * span] = contract(
            query_grad, weights(1, i, 0, head), 1, 1
        )
    later_state = collect(1)
    key_grad = key_part + contract(value_rows, later_state, 1, 1)
    value_grad = value_part + jnp.dot(key_rows, later_state, preferred_element_type=jnp.float32)
    joined = jnp.concatenate([key_grad, value_grad], axis=-1).astype(jnp.bfloat16)
    outs = []
    for i in range(parts):
        cols = pl.ds(i * span, span)
        ob[:, i * span : (i + 1) * span] = (
            contract(joined, weights(0, i, 0, 2 * head), 1, 1)
            + query_out[:, i * span : (i + 1) * span]
        ).astype(jnp.bfloat16)
        copy = pltpu.make_async_copy(ob.at[:, cols], out_hbm.at[:, cols], out_sem.at[i])
        copy.start()
        outs.append(copy)
    for copy, cond in sent + state_waits:
        if cond is None:
            copy.wait_send()
        else:
            pl.when(cond)(copy.wait_send)
    for copy in outs:
        copy.wait()


def per_device_fused(devices, planes, inputs, w_project, w_output, norm_gain, out_grad):
    tokens, grads_in = inputs[0], out_grad[0]
    count, width = tokens.shape
    rows, _, head = w_project.shape
    bf16, f32 = jnp.bfloat16, jnp.float32
    chips = devices // CORES
    hops = max(planes - 1, 1)
    dma = pltpu.SemaphoreType.DMA
    any_spec = pl.BlockSpec(memory_space=pl.ANY)
    result = pl.pallas_call(
        functools.partial(fused_kernel, planes),
        out_shape=jax.ShapeDtypeStruct((count, width), bf16),
        in_specs=[pl.BlockSpec(memory_space=pltpu.HBM)] * 4 + [pl.BlockSpec(memory_space=pltpu.VMEM)],
        out_specs=any_spec,
        scratch_shapes=[
            pltpu.VMEM((count, width), bf16),
            pltpu.VMEM((count, width), bf16),
            pltpu.VMEM((PIECES, devices, rows, 2 * head), bf16),
            pltpu.VMEM((count, width), bf16),
            pltpu.VMEM((PIECES, count, 2 * head), f32),
            pltpu.VMEM((count, width), f32),
            pltpu.VMEM((2, head, head), bf16),
            pltpu.VMEM((2, 4, head, head), bf16),
            pltpu.VMEM((2, head, head), bf16),
            pltpu.VMEM((2, hops, head, head), bf16),
            pltpu.VMEM((head, head), f32),
            dma((2,)),
            dma((4,)),
            dma((4,)),
            dma((2, PIECES, PARTS, chips)),
            dma((5, PIECES, PARTS, chips)),
            dma((2, 4)),
            dma((2, 4)),
            dma((2, hops)),
            dma((2, hops)),
        ],
        compiler_params=pltpu.CompilerParams(
            collective_id=0, has_side_effects=True, vmem_limit_bytes=67043328
        ),
    )(tokens, grads_in, jnp.transpose(w_project, (1, 0, 2)), w_output, norm_gain.reshape(1, head))
    return result[None]


def per_device(ndp, nseq, inputs, w_project, w_output, norm_gain, out_grad):
    rows, head = w_project.shape[0], w_project.shape[2]
    fits = (
        ndp == 2
        and nseq % (CORES * WIDE) == 0
        and inputs.shape[0] == 1
        and rows % 16 == 0
        and (ndp * nseq // 4 * rows) % 128 == 0
        and head % 128 == 0
    )
    if not fits:
        return per_device_plain(inputs, w_project, w_output, norm_gain, out_grad)
    return per_device_fused(
        ndp * nseq, nseq // (CORES * WIDE), inputs, w_project, w_output, norm_gain, out_grad
    )


def solution(mesh):
    in_specs = (
        P("dp", "seq", None),
        P(("dp", "seq"), None, None),
        P(("dp", "seq"), None),
        P(),
        P("dp", "seq", None),
    )
    out_specs = P("dp", "seq", None)
    return jax.shard_map(
        functools.partial(per_device, mesh.shape["dp"], mesh.shape["seq"]),
        mesh=mesh, in_specs=in_specs, out_specs=out_specs, check_vma=False
    )
```

```python
import functools

import jax
import jax.numpy as jnp
from jax import lax
from jax.experimental import pallas as pl
from jax.experimental.pallas import tpu as pltpu
from jax.sharding import PartitionSpec as P


def contract(left, right, left_dim, right_dim):
    return lax.dot_general(
        left, right, (((left_dim,), (right_dim,)), ((), ())), preferred_element_type=jnp.float32
    )


def other_blocks(local, reverse):
    every = lax.all_gather(local[None].astype(jnp.bfloat16), "seq", axis=0, tiled=True).astype(
        jnp.float32
    )
    own_index = lax.axis_index("seq")
    rank_list = jnp.arange(every.shape[0], dtype=jnp.int32)
    if reverse:
        selected = rank_list > own_index
    else:
        selected = rank_list < own_index
    return jnp.sum(jnp.where(selected[:, None, None], every, 0.0), axis=0)


def per_device_plain(inputs, w_project, w_output, norm_gain, out_grad):
    proj_full, out_full = (
        lax.all_gather(w_project, ("dp", "seq"), axis=0, tiled=True),
        lax.all_gather(w_output, ("dp", "seq"), axis=0, tiled=True),
    )
    width = proj_full.shape[0]
    head = proj_full.shape[2]
    flat_proj = proj_full.reshape(width, 3 * head)
    tokens = inputs[0]
    grads_in = out_grad[0]
    count = tokens.shape[0]
    projected = jnp.dot(tokens, flat_proj, preferred_element_type=jnp.float32).astype(jnp.bfloat16)
    queries = projected[:, :head]
    key_rows = projected[:, head : 2 * head]
    value_rows = projected[:, 2 * head :]
    row_ids = lax.broadcasted_iota(jnp.int32, (count, count), 0)
    col_ids = lax.broadcasted_iota(jnp.int32, (count, count), 1)
    causal = row_ids >= col_ids
    scores = jnp.where(causal, contract(queries, key_rows, 1, 1), 0.0).astype(jnp.bfloat16)
    intra_part = jnp.dot(scores, value_rows, preferred_element_type=jnp.float32)
    local_state = contract(key_rows, value_rows, 0, 0)
    prior_state = other_blocks(local_state, False).astype(jnp.bfloat16)
    attended = intra_part + jnp.dot(queries, prior_state, preferred_element_type=jnp.float32)
    inv_rms = lax.rsqrt(jnp.mean(attended * attended, axis=-1, keepdims=True) + 1e-06)
    head_grad = jnp.dot(grads_in, out_full, preferred_element_type=jnp.float32)
    scaled = norm_gain * head_grad
    attn_grad = inv_rms * scaled - attended * inv_rms**3 * jnp.mean(
        attended * scaled, axis=-1, keepdims=True
    )
    attn_grad = attn_grad.astype(jnp.bfloat16)
    prob_grad = jnp.where(causal, contract(attn_grad, value_rows, 1, 1), 0.0).astype(jnp.bfloat16)
    local_grad = contract(queries, attn_grad, 0, 0)
    later_state = other_blocks(local_grad, True).astype(jnp.bfloat16)
    query_grad = jnp.dot(prob_grad, key_rows, preferred_element_type=jnp.float32) + contract(
        attn_grad, prior_state, 1, 1
    )
    key_grad = contract(prob_grad, queries, 0, 0) + contract(value_rows, later_state, 1, 1)
    value_grad = contract(scores, attn_grad, 0, 0) + jnp.dot(
        key_rows, later_state, preferred_element_type=jnp.float32
    )
    joined = jnp.concatenate([query_grad, key_grad, value_grad], axis=-1).astype(jnp.bfloat16)
    result = contract(joined, flat_proj, 1, 1).astype(jnp.bfloat16)
    return result[None]


CORES = 2
WIDE = 2
PIECES = 2
ROUTED = 1
PARTS = 1
MESH = pl.DeviceIdType.MESH
FIRST, UP, DOWN, LAST, CORE = range(5)


def fused_kernel(
    planes, x_hbm, g_hbm, w_hbm, o_hbm, gain_ref, out_hbm,
    xv, gv, wbuf, ob, proj, query_out, st_send, st_in, sum_send, sum_in, acc,
    load_sem, own_sem, out_sem, recv_sem, send_sem, st_rs, st_ss, sum_rs, sum_ss,
):
    y = lax.axis_index("dp")
    seq = lax.axis_index("seq")
    core = seq % CORES
    x = (seq // CORES) % WIDE
    z = seq // (CORES * WIDE)
    head = st_send.shape[-1]
    count, width = xv.shape
    devices = wbuf.shape[1]
    rows = wbuf.shape[2]
    ya, xa = (y + core) % 2, (x + 1 - core) % 2
    yb, xb = (y + 1 - core) % 2, (x + core) % 2

    def dev(yy, zz, xx, cc):
        return (yy, (zz * WIDE + xx) * CORES + cc)

    def chip(yy, zz, xx):
        return (yy * planes + zz) * WIDE + xx

    x_load = pltpu.make_async_copy(x_hbm, xv, load_sem.at[0])
    g_load = pltpu.make_async_copy(g_hbm, gv, load_sem.at[1])
    me = chip(y, z, x) * CORES + core
    own = [
        [
            pltpu.make_async_copy(
                w_hbm.at[1 + j], wbuf.at[0, me, :, pl.ds(j * head, head)], own_sem.at[3 * j]
            )
            for j in range(2)
        ],
        [
            pltpu.make_async_copy(
                w_hbm.at[0], wbuf.at[1, me, :, pl.ds(0, head)], own_sem.at[1]
            ),
            pltpu.make_async_copy(o_hbm, wbuf.at[1, me, :, pl.ds(head, head)], own_sem.at[2]),
        ],
    ]
    for copies in own:
        for copy in copies:
            copy.start()
    x_load.start()
    g_load.start()

    barrier = pltpu.get_barrier_semaphore()
    near = [
        dev(y, z, x, 1 - core),
        dev(y, z, 1 - x, core),
        dev(y, z, 1 - x, 1 - core),
        dev(1 - y, z, x, core),
    ] + [dev(y, (z + dz) % planes, x, core) for dz in range(1, planes)]
    for other in near:
        pl.semaphore_signal(barrier, inc=1, device_id=other, device_id_type=MESH)
    pl.semaphore_wait(barrier, len(near))

    spans = (pl.ds(0, rows),)

    def shard_copy(way, p, part, origin, owner, target):
        slot = wbuf.at[p, origin * CORES + owner, spans[part]]
        return pltpu.make_async_remote_copy(
            src_ref=slot,
            dst_ref=slot,
            send_sem=send_sem.at[way, p, part, origin],
            recv_sem=recv_sem.at[1 if way == CORE else 0, p, part, origin],
            device_id=target,
            device_id_type=MESH,
        )

    targets = [
        dev(ya, z, xa, core),
        dev(y, lax.rem(z + 1, planes), x, core),
        dev(y, lax.rem(z + planes - 1, planes), x, core),
        dev(yb, z, xb, core),
        dev(y, z, x, 1 - core),
    ]
    sent = []

    def send(way, p, part, origin, cond=None):
        copy = shard_copy(way, p, part, origin, core, targets[way])
        sent.append((copy, cond))
        if cond is None:
            copy.start()
        else:
            pl.when(cond)(copy.start)

    def arrive(p, part, origin, valid=None):
        wait = shard_copy(FIRST, p, part, origin, core, targets[FIRST]).wait_recv
        if valid is None:
            wait()
        else:
            pl.when(valid)(wait)

    up, down = z < planes - 1, z > 0

    def both_ways(k):
        if k == 0:
            return [(z, None, None)]
        return [(z - k, z - k >= 0, 1), (z + k, z + k < planes, -1)]

    def begin(p):
        for copy in own[p]:
            copy.wait()
        mine = chip(y, z, x)
        for part in range(PARTS):
            send(UP, p, part, mine, up)
            send(DOWN, p, part, mine, down)
            send(FIRST, p, part, mine)
        for part in range(PARTS):
            send(LAST, p, part, mine)
            send(CORE, p, part, mine)

    def step(p, k):
        if k == 0:
            other = chip(ya, z, xa)
            for part in range(ROUTED):
                arrive(p, part, other)
                send(UP, p, part, other, up)
                send(DOWN, p, part, other, down)
                send(LAST, p, part, other)
                send(CORE, p, part, other)
            return
        for part, (yy, xx) in [(part, (y, x)) for part in range(PARTS)] + [
            (part, (ya, xa)) for part in range(ROUTED)
        ]:
            for zz, valid, sign in both_ways(k):
                origin = chip(yy, zz, xx)
                arrive(p, part, origin, valid)
                if sign == 1:
                    send(UP, p, part, origin, jnp.logical_and(valid, up))
                else:
                    send(DOWN, p, part, origin, jnp.logical_and(valid, down))
                if part >= ROUTED:
                    send(FIRST, p, part, origin, valid)
                send(LAST, p, part, origin, valid)
                send(CORE, p, part, origin, valid)

    def across(p, k):
        for part, (yy, xx) in [(part, (yb, xb)) for part in range(PARTS)] + [
            (part, (1 - y, 1 - x)) for part in range(ROUTED)
        ]:
            for zz, valid, _ in both_ways(k):
                origin = chip(yy, zz, xx)
                arrive(p, part, origin, valid)
                send(CORE, p, part, origin, valid)

    def settle(p, k):
        for zz, valid, _ in both_ways(k):

            def finish():
                for yy in range(2):
                    for xx in range(WIDE):
                        for part in range(PARTS):
                            shard_copy(
                                CORE, p, part, chip(yy, zz, xx), 1 - core, targets[CORE]
                            ).wait_recv()
                project(p, zz, k == 0)

            if valid is None:
                finish()
            else:
                pl.when(valid)(finish)

    def project(p, zz, first):
        if first:
            (x_load, g_load)[p].wait()
        terms = []
        for yy in range(2):
            base = (yy * planes + zz) * WIDE * CORES
            cols = pl.ds(pl.multiple_of(base * rows, 128), WIDE * CORES * rows)
            block = wbuf[p, pl.ds(base, WIDE * CORES)].reshape(WIDE * CORES * rows, 2 * head)
            if p == 0:
                terms.append(jnp.dot(xv[:, cols], block, preferred_element_type=jnp.float32))
            else:
                terms.append(
                    jnp.concatenate(
                        [
                            jnp.dot(
                                xv[:, cols], block[:, :head], preferred_element_type=jnp.float32
                            ),
                            jnp.dot(
                                gv[:, cols], block[:, head:], preferred_element_type=jnp.float32
                            ),
                        ],
                        axis=-1,
                    )
                )
        total = terms[0] + terms[1]
        proj[p] = total if first else proj[p] + total

    parts = 4 if devices % 4 == 0 else 1
    group = devices // parts
    span = group * rows

    def weights(p, i, low, high):
        block = wbuf[p, i * group : (i + 1) * group]
        return block.reshape(span, 2 * head)[:, low:high]

    place = x * CORES + core
    state_waits = []

    def plane_peer(j):
        return (x + j // 2) % 2, (core + j % 2) % 2

    def spread(e, local):
        st_send[e] = local.astype(jnp.bfloat16)
        for j in (2, 3, 1):
            px, pc = plane_peer(j)
            copy = pltpu.make_async_remote_copy(
                src_ref=st_send.at[e],
                dst_ref=st_in.at[e, place],
                send_sem=st_ss.at[e, j],
                recv_sem=st_rs.at[e, place],
                device_id=dev(y, z, px, pc),
                device_id_type=MESH,
            )
            copy.start()
            state_waits.append((copy, None))

    def plane_sum(e, local):
        total = local
        partial = jnp.zeros_like(local)
        for j in range(1, 4):
            px, pc = plane_peer(j)
            index = px * CORES + pc
            pltpu.make_async_remote_copy(
                src_ref=st_send.at[e],
                dst_ref=st_in.at[e, index],
                send_sem=st_ss.at[e, j],
                recv_sem=st_rs.at[e, index],
                device_id=dev(y, z, px, pc),
                device_id_type=MESH,
            ).wait_recv()
            block = st_in[e, index].astype(jnp.float32)
            total = total + block
            chosen = (index < place) if e == 0 else (index > place)
            partial = partial + jnp.where(chosen, block, 0.0)
        acc[...] = partial
        sum_send[e] = total.astype(jnp.bfloat16)
        for dz in range(planes - 1, 0, -1):
            zz = z + dz if e == 0 else z - dz
            valid = (zz < planes) if e == 0 else (zz >= 0)
            copy = pltpu.make_async_remote_copy(
                src_ref=sum_send.at[e],
                dst_ref=sum_in.at[e, dz - 1],
                send_sem=sum_ss.at[e, dz - 1],
                recv_sem=sum_rs.at[e, dz - 1],
                device_id=dev(y, zz, x, core),
                device_id_type=MESH,
            )
            pl.when(valid)(copy.start)
            state_waits.append((copy, valid))

    def collect(e):
        for dz in range(1, planes):
            valid = (z - dz >= 0) if e == 0 else (z + dz < planes)

            @pl.when(valid)
            def _():
                pltpu.make_async_remote_copy(
                    src_ref=sum_send.at[e],
                    dst_ref=sum_in.at[e, dz - 1],
                    send_sem=sum_ss.at[e, dz - 1],
                    recv_sem=sum_rs.at[e, dz - 1],
                    device_id=targets[CORE],
                    device_id_type=MESH,
                ).wait_recv()
                acc[...] += sum_in[e, dz - 1].astype(jnp.float32)

        return acc[...].astype(jnp.bfloat16)

    for p in range(PIECES):
        begin(p)
    order = [(0, 0)]
    for k in range(1, planes):
        order += [(0, k), (1, k - 1)]
    order.append((1, planes - 1))
    keyval_at = order.index((0, planes - 1)) + 2
    for i in range(len(order) + 2):
        if i < len(order):
            step(*order[i])
        if 1 <= i <= len(order):
            across(*order[i - 1])
        if i == keyval_at + 1:
            plane_sum(0, local_state)
        if i >= 2:
            settle(*order[i - 2])
        if i == keyval_at:
            kv = proj[0].astype(jnp.bfloat16)
            key_rows, value_rows = kv[:, :head], kv[:, head:]
            local_state = contract(key_rows, value_rows, 0, 0)
            spread(0, local_state)

    queries = proj[1, :, :head].astype(jnp.bfloat16)
    head_grad = proj[1, :, head:]
    row_ids = lax.broadcasted_iota(jnp.int32, (count, count), 0)
    col_ids = lax.broadcasted_iota(jnp.int32, (count, count), 1)
    causal = row_ids >= col_ids
    scores = jnp.where(causal, contract(queries, key_rows, 1, 1), 0.0).astype(jnp.bfloat16)
    intra_part = jnp.dot(scores, value_rows, preferred_element_type=jnp.float32)
    scaled = gain_ref[...] * head_grad
    prior_state = collect(0)
    attended = intra_part + jnp.dot(queries, prior_state, preferred_element_type=jnp.float32)
    inv_rms = lax.rsqrt(jnp.mean(attended * attended, axis=-1, keepdims=True) + 1e-06)
    attn_grad = inv_rms * scaled - attended * (inv_rms * inv_rms * inv_rms) * jnp.mean(
        attended * scaled, axis=-1, keepdims=True
    )
    attn_grad = attn_grad.astype(jnp.bfloat16)
    local_grad = contract(queries, attn_grad, 0, 0)
    spread(1, local_grad)
    prob_grad = jnp.where(causal, contract(attn_grad, value_rows, 1, 1), 0.0).astype(jnp.bfloat16)
    query_grad = jnp.dot(prob_grad, key_rows, preferred_element_type=jnp.float32) + contract(
        attn_grad, prior_state, 1, 1
    )
    query_grad = query_grad.astype(jnp.bfloat16)
    plane_sum(1, local_grad)
    key_part = contract(prob_grad, queries, 0, 0)
    value_part = contract(scores, attn_grad, 0, 0)
    for i in range(parts):
        query_out[:, i * span : (i + 1) * span] = contract(
            query_grad, weights(1, i, 0, head), 1, 1
        )
    later_state = collect(1)
    key_grad = key_part + contract(value_rows, later_state, 1, 1)
    value_grad = value_part + jnp.dot(key_rows, later_state, preferred_element_type=jnp.float32)
    joined = jnp.concatenate([key_grad, value_grad], axis=-1).astype(jnp.bfloat16)
    outs = []
    for i in range(parts):
        cols = pl.ds(i * span, span)
        ob[:, i * span : (i + 1) * span] = (
            contract(joined, weights(0, i, 0, 2 * head), 1, 1)
            + query_out[:, i * span : (i + 1) * span]
        ).astype(jnp.bfloat16)
        copy = pltpu.make_async_copy(ob.at[:, cols], out_hbm.at[:, cols], out_sem.at[i])
        copy.start()
        outs.append(copy)
    for copy, cond in sent + state_waits:
        if cond is None:
            copy.wait_send()
        else:
            pl.when(cond)(copy.wait_send)
    for copy in outs:
        copy.wait()


def per_device_fused(devices, planes, inputs, w_project, w_output, norm_gain, out_grad):
    tokens, grads_in = inputs[0], out_grad[0]
    count, width = tokens.shape
    rows, _, head = w_project.shape
    bf16, f32 = jnp.bfloat16, jnp.float32
    chips = devices // CORES
    hops = max(planes - 1, 1)
    dma = pltpu.SemaphoreType.DMA
    any_spec = pl.BlockSpec(memory_space=pl.ANY)
    result = pl.pallas_call(
        functools.partial(fused_kernel, planes),
        out_shape=jax.ShapeDtypeStruct((count, width), bf16),
        in_specs=[pl.BlockSpec(memory_space=pltpu.HBM)] * 4 + [pl.BlockSpec(memory_space=pltpu.VMEM)],
        out_specs=any_spec,
        scratch_shapes=[
            pltpu.VMEM((count, width), bf16),
            pltpu.VMEM((count, width), bf16),
            pltpu.VMEM((PIECES, devices, rows, 2 * head), bf16),
            pltpu.VMEM((count, width), bf16),
            pltpu.VMEM((PIECES, count, 2 * head), f32),
            pltpu.VMEM((count, width), f32),
            pltpu.VMEM((2, head, head), bf16),
            pltpu.VMEM((2, 4, head, head), bf16),
            pltpu.VMEM((2, head, head), bf16),
            pltpu.VMEM((2, hops, head, head), bf16),
            pltpu.VMEM((head, head), f32),
            dma((2,)),
            dma((4,)),
            dma((4,)),
            dma((2, PIECES, PARTS, chips)),
            dma((5, PIECES, PARTS, chips)),
            dma((2, 4)),
            dma((2, 4)),
            dma((2, hops)),
            dma((2, hops)),
        ],
        compiler_params=pltpu.CompilerParams(
            collective_id=0, has_side_effects=True, vmem_limit_bytes=67043328
        ),
    )(tokens, grads_in, jnp.transpose(w_project, (1, 0, 2)), w_output, norm_gain.reshape(1, head))
    return result[None]


def per_device(ndp, nseq, inputs, w_project, w_output, norm_gain, out_grad):
    rows, head = w_project.shape[0], w_project.shape[2]
    fits = (
        ndp == 2
        and nseq % (CORES * WIDE) == 0
        and inputs.shape[0] == 1
        and rows % 16 == 0
        and (ndp * nseq // 4 * rows) % 128 == 0
        and head % 128 == 0
    )
    if not fits:
        return per_device_plain(inputs, w_project, w_output, norm_gain, out_grad)
    return per_device_fused(
        ndp * nseq, nseq // (CORES * WIDE), inputs, w_project, w_output, norm_gain, out_grad
    )


def solution(mesh):
    in_specs = (
        P("dp", "seq", None),
        P(("dp", "seq"), None, None),
        P(("dp", "seq"), None),
        P(),
        P("dp", "seq", None),
    )
    out_specs = P("dp", "seq", None)
    return jax.shard_map(
        functools.partial(per_device, mesh.shape["dp"], mesh.shape["seq"]),
        mesh=mesh, in_specs=in_specs, out_specs=out_specs, check_vma=False
    )
```
